256 devices in a mesh: space: 32 (over x, y, core), mem: 8 (over z).
Axes of the slice: x: 4, y: 4, z: 8, core: 2. Of those that a mesh axis runs over, the one named last changes fastest.
Arguments:
- increment: float32 [16, 262144], P(None, 'space'), may hold values from -6 to 6
- anomalies: bfloat16 [64, 16, 262144], P('mem', None, 'space'), may hold values from -6 to 6
- interp_index: int32 [3, 262144], P(None, 'space'), may hold values from 0 to 2302, as said below
- interp_weight: float32 [3, 262144], P(None, 'space'), may hold values from 0.2 to 1
- neighbour_blocks: int32 [9, 512], P(None, 'space'), may hold values from 0 to 31, as said below
- tiles: bfloat16 [512, 9, 128, 128], P('space'), may hold values from -0.1875 to 0.1875
Outputs:
- covariance_image: float32 [16, 262144], P(None, ('space', 'mem'))
The draws below stay inside these ranges and needn't reach their ends.
Inputs may be any that keep to these rules, and one draw needn't show every extreme that they name: `interp_index`: column j of a patch, at position i = j % 8192, names points from c - 128 to c + 127, where c = 128 + i * 2048 // 8192. `neighbour_blocks`: row 0 names the block itself (8 plus its place in the patch); the others lie within 8 blocks of it.
All inputs are finite; a program needn't handle non-finite values.
Results may differ from the reference program's by a relative error of at most 0.015.
Values may be sent and summed in bfloat16 or wider, within the bound.
A program may use at most 64 MiB of HBM per device.

```python
import jax
import jax.numpy as jnp
from jax import lax

LEV = 8
VAR = 2
COLS_DEV = 8192
BLOCK = 128
NB = 9
HI = 128
INTP = 3
SUB_DEV = 2048
HB = 8
HS = 1024
MEMBERS = 64
COLS = 262144
SUBS = 65536
NBLKS = 512


def draw_interp_index(key, part):
    position = jnp.arange(COLS, dtype=jnp.int32) % COLS_DEV
    centre = HI + position * SUB_DEV // COLS_DEV
    offset = jax.random.randint(key, (INTP, COLS), -HI, HI, dtype=jnp.int32)
    return (centre[None, :] + offset).astype(jnp.int32)


def draw_neighbour_blocks(key, part):
    itself = jnp.arange(NBLKS, dtype=jnp.int32) % (SUB_DEV // BLOCK) + HB
    offset = jax.random.randint(key, (NB, NBLKS), -HB, HB + 1, dtype=jnp.int32)
    offset = offset.at[0].set(0)
    return (itself[None, :] + offset).astype(jnp.int32)


def block_levels(stream_key, shape, split, smallest, high):
    loudness = 1.0
    for axis_at, parts in split:
        heights = jax.random.uniform(jax.random.fold_in(jax.random.fold_in(stream_key, 6), axis_at), (parts,), jnp.float32, smallest / len(split), high / len(split))
        loudness = loudness * jnp.repeat(jnp.exp(heights), shape[axis_at] // parts).reshape((-1,) + (1,) * (len(shape) - 1 - axis_at))
    return loudness


def scatter_about(stream_key, dims, deviation, reach, shards=(), kind=jnp.bfloat16):
    drawn = deviation * jax.random.normal(stream_key, dims, jnp.float32)
    if shards:
        drawn = drawn * block_levels(stream_key, dims, shards, -0.22, 0.18)
    return jnp.clip(drawn, -reach, reach).astype(kind)


def setup_inputs(seed: int = 0) -> dict:
    seeds = jax.random.split(jax.random.key(seed), 7)
    return {
        "increment": scatter_about(seeds[0], (LEV * VAR, COLS), 1.0, 6.0, ((1, 32),), jnp.float32),
        "anomalies": scatter_about(seeds[1], (MEMBERS, LEV * VAR, COLS), 1.0, 6.0, ((0, 8), (2, 32))),
        "interp_index": draw_interp_index(jax.random.fold_in(seeds[6], 71), 0),
        "interp_weight": jnp.clip(0.2 + 0.8 * jax.random.uniform(seeds[3], (INTP, COLS), jnp.float32) ** block_levels(seeds[3], (INTP, COLS), ((1, 32),), -0.2, 0.2), 0.2, 1.0),
        "neighbour_blocks": draw_neighbour_blocks(jax.random.fold_in(seeds[6], 71), 0),
        "tiles": scatter_about(seeds[5], (NBLKS, NB, BLOCK, BLOCK), (NB * BLOCK) ** -0.5, 0.1875, ((0, 32),)),
    }


def reference(increment, anomalies, interp_index, interp_weight, neighbour_blocks, tiles):
    n_fields = increment.shape[0]
    blocks_dev = SUB_DEV // BLOCK
    column_patch = jnp.arange(COLS, dtype=jnp.int32) // COLS_DEV
    point_index = (column_patch[None, :] * SUB_DEV + interp_index).astype(jnp.int32)
    block_patch = jnp.arange(NBLKS, dtype=jnp.int32) // blocks_dev
    block_index = (block_patch[None, :] * blocks_dev + neighbour_blocks).astype(jnp.int32)
    tiles_wide = tiles.astype(jnp.float32)

    def member(summed, anomaly):
        weighted = anomaly.astype(jnp.float32) * increment
        spread = jnp.zeros((n_fields, SUBS + 2 * HI), jnp.float32)
        spread = spread.at[:, point_index].add(weighted[:, None, :] * interp_weight[None])
        sub_values = spread[:, HI:HI + SUBS].astype(jnp.bfloat16)
        padded = jnp.pad(sub_values, ((0, 0), (HS, HS)))
        blocked = padded.reshape(n_fields, NBLKS + 2 * HB, BLOCK)
        picked = blocked[:, block_index, :].astype(jnp.float32)
        smooth = jnp.einsum("fnbk,bnkl->fbl", picked, tiles_wide, precision=lax.Precision.HIGHEST)
        smooth = smooth.reshape(n_fields, SUBS).astype(jnp.bfloat16)
        widened = jnp.pad(smooth, ((0, 0), (HI, HI)))
        returned = jnp.sum(widened[:, point_index].astype(jnp.float32) * interp_weight[None], axis=1)
        return summed + anomaly.astype(jnp.float32) * returned, None

    start = jnp.zeros((n_fields, COLS), jnp.float32)
    summed, unused = lax.scan(member, start, anomalies)
    return summed / (MEMBERS - 1)
```

```python
import jax
import jax.numpy as jnp
from jax import lax
from jax.experimental import pallas as pl
from jax.experimental.pallas import tpu as pltpu
from jax.sharding import PartitionSpec as P

MESH = pl.DeviceIdType.MESH
BLOCK = 128
INTP = 3
SUB_DEV = 2048
NB = 9
HB = 8
CB = 512
NCB = 16
WIN = 384
GREET = 2
F32 = jnp.float32
BF16 = jnp.bfloat16


def dedupe(i0, i1, i2, w0, w1, w2):
    same01, same02, same12 = i0 == i1, i0 == i2, i1 == i2
    zero = jnp.zeros_like(w0)
    none = jnp.full_like(i0, 512.0)
    w0 = w0 + jnp.where(same01, w1, zero) + jnp.where(same02, w2, zero)
    w1 = w1 + jnp.where(same12, w2, zero)
    return i0, jnp.where(same01, none, i1), jnp.where(same02 | same12, none, i2), w0, w1, w2


def build_table(cb, idx_v, wgt_v, table):
    iota = lax.broadcasted_iota(jnp.int32, (16, BLOCK), 0).astype(F32)
    for t in range(CB // BLOCK):
        cols = pl.ds(pl.multiple_of(cb * CB + t * BLOCK, BLOCK), BLOCK)
        idx = [(idx_v[k : k + 1, cols] - (cb * BLOCK + WIN // 2)).astype(F32) for k in range(INTP)]
        wgt = [wgt_v[k : k + 1, cols] for k in range(INTP)]
        rows = [jnp.broadcast_to(v, (16, BLOCK)).astype(BF16) for v in dedupe(*idx, *wgt)]
        i0, i1, i2, w0, w1, w2 = rows
        for r in range(WIN // 16):
            if r * 16 + 16 <= 32 * t or r * 16 >= 32 * t + 288:
                val = jnp.zeros((16, BLOCK), BF16)
            else:
                point = (iota + (r * 16 - WIN // 2)).astype(BF16)
                val = jnp.where(i2 == point, w2, jnp.zeros((16, BLOCK), BF16))
                val = jnp.where(i1 == point, w1, val)
                val = jnp.where(i0 == point, w0, val)
            table[r * 16 : r * 16 + 16, t * BLOCK : (t + 1) * BLOCK] = val


def kernel(
    n_space,
    n_mem,
    inc_h,
    anom_h,
    idx_h,
    wgt_h,
    nb_h,
    tiles_h,
    out_ref,
    inc_v,
    anom_v,
    idx_v,
    wgt_v,
    nb_s,
    tiles_v,
    table_l,
    table_r,
    carry_l,
    carry_r,
    edge,
    spread,
    recv_l,
    recv_r,
    sub,
    smooth,
    part,
    zrecv,
    own,
    in_sem,
    anom_sem,
    tile_sem,
    send_l_sem,
    send_r_sem,
    recv_l_sem,
    recv_r_sem,
    smooth_send_sem,
    smooth_recv_sem,
    z_send_sem,
    z_recv_sem,
):
    me = lax.axis_index("space")
    z = lax.axis_index("mem")
    left, right = me - 1, me + 1
    has_left, has_right = me > 0, me < n_space - 1
    half = NCB // 2

    loads = [
        pltpu.make_async_copy(idx_h, idx_v, in_sem.at[0]),
        pltpu.make_async_copy(wgt_h, wgt_v, in_sem.at[1]),
        pltpu.make_async_copy(inc_h, inc_v, in_sem.at[2]),
        pltpu.make_async_copy(nb_h, nb_s, in_sem.at[3]),
    ]
    for c in loads:
        c.start()

    def anom_copy(cb):
        cols = pl.ds(pl.multiple_of(cb * CB, CB), CB)
        return pltpu.make_async_copy(anom_h.at[:, cols], anom_v.at[:, cols], anom_sem.at[cb])

    for k in range(half):
        anom_copy(k).start()
        anom_copy(NCB - 1 - k).start()

    def tile_copy(b):
        return pltpu.make_async_copy(tiles_h.at[b], tiles_v.at[b], tile_sem.at[b])

    for d in range(half):
        tile_copy(half - 1 - d).start()
        tile_copy(half + d).start()

    barrier = pltpu.get_barrier_semaphore()

    @pl.when(has_left)
    def _():
        pl.semaphore_signal(barrier, inc=1, device_id={"space": left}, device_id_type=MESH)

    @pl.when(has_right)
    def _():
        pl.semaphore_signal(barrier, inc=1, device_id={"space": right}, device_id_type=MESH)

    for off in range(1, n_mem):
        pl.semaphore_signal(
            barrier, inc=1, device_id={"mem": lax.rem(z + off, n_mem)}, device_id_type=MESH
        )

    def to_left(k):
        return pltpu.make_async_remote_copy(
            src_ref=spread.at[k],
            dst_ref=recv_r.at[k],
            send_sem=send_l_sem.at[k],
            recv_sem=recv_r_sem.at[k],
            device_id={"space": left},
            device_id_type=MESH,
        )

    def to_right(k):
        return pltpu.make_async_remote_copy(
            src_ref=spread.at[17 - k],
            dst_ref=recv_l.at[k],
            send_sem=send_r_sem.at[k],
            recv_sem=recv_l_sem.at[k],
            device_id={"space": right},
            device_id_type=MESH,
        )

    def send_pair(k):
        @pl.when(has_left)
        def _():
            to_left(k).start()

        @pl.when(has_right)
        def _():
            to_right(k).start()

    for c in loads:
        c.wait()
    carry_l[...] = jnp.zeros_like(carry_l)
    carry_r[...] = jnp.zeros_like(carry_r)

    def spread_window(cb, table):
        cols = pl.ds(pl.multiple_of(cb * CB, CB), CB)
        inc = inc_v[:, cols].astype(BF16)
        weighted = (anom_v[:, cols].reshape(8, 16, CB) * inc[None]).reshape(128, CB)
        return lax.dot_general(
            weighted, table[...], (((1,), (1,)), ((), ())), preferred_element_type=F32
        )

    def spread_step(k, greet):
        cl, cr = k, NCB - 1 - k
        anom_copy(cl).wait()
        anom_copy(cr).wait()
        build_table(cl, idx_v, wgt_v, table_l.at[k])
        build_table(cr, idx_v, wgt_v, table_r.at[k])
        win_l = spread_window(cl, table_l.at[k])
        win_r = spread_window(cr, table_r.at[k])
        done_l = win_l[:, :128] + carry_l[0]
        done_r = win_r[:, 256:] + carry_r[0]
        carry_l[0] = win_l[:, 128:256] + carry_l[1]
        carry_r[0] = win_r[:, 128:256] + carry_r[1]
        carry_l[1] = win_l[:, 256:]
        carry_r[1] = win_r[:, :128]
        spread[k] = done_l.astype(BF16)
        spread[17 - k] = done_r.astype(BF16)
        return done_l, done_r

    for k in range(GREET):
        done_l, done_r = spread_step(k, False)
        if k < 2:
            edge[k] = done_l
            edge[3 - k] = done_r

    pl.semaphore_wait(barrier, n_mem - 1 + has_left.astype(jnp.int32) + has_right.astype(jnp.int32))

    for k in range(GREET):
        send_pair(k)

    def spread_loop(k, carry):
        done_l, done_r = spread_step(k, False)
        sub[7 + k] = done_l.astype(BF16)
        sub[24 - k] = done_r.astype(BF16)
        send_pair(k)
        return carry

    lax.fori_loop(GREET, half, spread_loop, 0)
    mid_l = (carry_l[0] + carry_r[1]).astype(BF16)
    mid_r = (carry_l[1] + carry_r[0]).astype(BF16)
    spread[8] = mid_l
    spread[9] = mid_r
    sub[15] = mid_l
    sub[16] = mid_r
    send_pair(8)

    def conv(b):
        tile_copy(b).wait()
        picked = jnp.concatenate([sub[nb_s[n, b]] for n in range(NB)], axis=1)
        value = jnp.dot(picked, tiles_v[b], preferred_element_type=F32)
        smooth[1 + b] = value.astype(BF16)

    def interp(cb, table):
        window = jnp.concatenate([smooth[cb], smooth[cb + 1], smooth[cb + 2]], axis=1)
        back = jnp.dot(window, table[...], preferred_element_type=F32)
        cols = pl.ds(pl.multiple_of(cb * CB, CB), CB)
        prod = back * anom_v[:, cols].astype(F32)
        total = jnp.sum(prod.reshape(8, 16, CB), axis=0)
        owner, h = cb // 2, lax.rem(cb, 2)
        part[cb] = total.astype(BF16)

        @pl.when(owner == z)
        def _():
            own[h] = total

        @pl.when(owner != z)
        def _():
            z_copy(cb).start()

    def z_copy(cb):
        owner, h = cb // 2, lax.rem(cb, 2)
        return pltpu.make_async_remote_copy(
            src_ref=part.at[cb],
            dst_ref=zrecv.at[z, h],
            send_sem=z_send_sem.at[cb],
            recv_sem=z_recv_sem.at[z, h],
            device_id={"mem": owner},
            device_id_type=MESH,
        )

    @pl.when(has_left)
    def _():
        to_right(0).wait_recv()
        sub[8] = (edge[1] + recv_l[0].astype(F32)).astype(BF16)
        to_right(1).wait_recv()
        sub[7] = (edge[0] + recv_l[1].astype(F32)).astype(BF16)

    @pl.when(jnp.logical_not(has_left))
    def _():
        sub[8] = edge[1].astype(BF16)
        sub[0:8] = jnp.zeros((8, 128, 128), BF16)

    @pl.when(has_right)
    def _():
        to_left(0).wait_recv()
        sub[23] = (edge[2] + recv_r[0].astype(F32)).astype(BF16)
        to_left(1).wait_recv()
        sub[24] = (edge[3] + recv_r[1].astype(F32)).astype(BF16)

    @pl.when(jnp.logical_not(has_right))
    def _():
        sub[23] = edge[2].astype(BF16)
        sub[24:32] = jnp.zeros((8, 128, 128), BF16)

    conv(half - 1)
    conv(half)

    def conv_loop(d, carry):
        @pl.when(has_left)
        def _():
            to_right(d).wait_recv()
            sub[8 - d] = recv_l[d]

        @pl.when(has_right)
        def _():
            to_left(d).wait_recv()
            sub[23 + d] = recv_r[d]

        conv(half - d)
        conv(half - 1 + d)
        return carry

    lax.fori_loop(2, half + 1, conv_loop, 0)

    smooth_left = pltpu.make_async_remote_copy(
        src_ref=smooth.at[1],
        dst_ref=smooth.at[17],
        send_sem=smooth_send_sem.at[0],
        recv_sem=smooth_recv_sem.at[0],
        device_id={"space": left},
        device_id_type=MESH,
    )
    smooth_right = pltpu.make_async_remote_copy(
        src_ref=smooth.at[16],
        dst_ref=smooth.at[0],
        send_sem=smooth_send_sem.at[1],
        recv_sem=smooth_recv_sem.at[1],
        device_id={"space": right},
        device_id_type=MESH,
    )

    @pl.when(has_left)
    def _():
        smooth_left.start()

    @pl.when(has_right)
    def _():
        smooth_right.start()

    def interp_loop(s, carry):
        k = half - 1 - s
        interp(k, table_l.at[k])
        interp(NCB - 1 - k, table_r.at[k])
        return carry

    lax.fori_loop(0, half - 1, interp_loop, 0)

    @pl.when(has_left)
    def _():
        smooth_right.wait_recv()

    @pl.when(has_right)
    def _():
        smooth_left.wait_recv()

    @pl.when(jnp.logical_not(has_left))
    def _():
        smooth[0] = jnp.zeros((128, 128), BF16)

    @pl.when(jnp.logical_not(has_right))
    def _():
        smooth[17] = jnp.zeros((128, 128), BF16)

    interp(0, table_l.at[0])
    interp(NCB - 1, table_r.at[0])

    @pl.when(has_left)
    def _():
        for k in range(9):
            to_left(k).wait_send()
        smooth_left.wait_send()

    @pl.when(has_right)
    def _():
        for k in range(9):
            to_right(k).wait_send()
        smooth_right.wait_send()

    def z_arrived(source, h):
        return pltpu.make_async_remote_copy(
            src_ref=part.at[0],
            dst_ref=zrecv.at[source, h],
            send_sem=z_send_sem.at[0],
            recv_sem=z_recv_sem.at[source, h],
            device_id={"mem": source},
            device_id_type=MESH,
        )

    for h in range(2):
        total = own[h]
        for off in range(1, n_mem):
            source = lax.rem(z + off, n_mem)
            z_arrived(source, h).wait_recv()
            total = total + zrecv[source, h].astype(F32)
        out_ref[:, h * CB : (h + 1) * CB] = total * (1.0 / (8 * n_mem - 1))

    for cb in range(NCB):
        @pl.when(cb // 2 != z)
        def _():
            z_copy(cb).wait_send()


def shards(increment, anomalies, interp_index, interp_weight, neighbour_blocks, tiles):
    n_space, n_mem = lax.axis_size("space"), lax.axis_size("mem")
    anomalies = anomalies.reshape(128, NCB * CB)
    tiles = tiles.reshape(16, NB * BLOCK, BLOCK)
    hbm = pl.BlockSpec(memory_space=pl.ANY)
    vmem = pltpu.VMEM
    dma = pltpu.SemaphoreType.DMA
    return pl.pallas_call(
        lambda *refs: kernel(n_space, n_mem, *refs),
        out_shape=jax.ShapeDtypeStruct((16, 2 * CB), F32),
        in_specs=[hbm] * 6,
        out_specs=pl.BlockSpec(memory_space=pltpu.VMEM),
        scratch_shapes=[
            vmem((16, NCB * CB), F32),
            vmem((128, NCB * CB), BF16),
            vmem((INTP, NCB * CB), jnp.int32),
            vmem((INTP, NCB * CB), F32),
            pltpu.SMEM((NB, 16), jnp.int32),
            vmem((16, NB * BLOCK, BLOCK), BF16),
            vmem((8, WIN, CB), BF16),
            vmem((8, WIN, CB), BF16),
            vmem((2, 128, 128), F32),
            vmem((2, 128, 128), F32),
            vmem((4, 128, 128), F32),
            vmem((18, 128, 128), BF16),
            vmem((9, 128, 128), BF16),
            vmem((9, 128, 128), BF16),
            vmem((32, 128, 128), BF16),
            vmem((18, 128, 128), BF16),
            vmem((NCB, 16, CB), BF16),
            vmem((8, 2, 16, CB), BF16),
            vmem((2, 16, CB), F32),
            dma((4,)),
            dma((NCB,)),
            dma((16,)),
            dma((9,)),
            dma((9,)),
            dma((9,)),
            dma((9,)),
            dma((2,)),
            dma((2,)),
            dma((NCB,)),
            dma((8, 2)),
        ],
        compiler_params=pltpu.CompilerParams(
            collective_id=0, has_side_effects=True, vmem_limit_bytes=67_043_328
        ),
        name="nicas",
    )(increment, anomalies, interp_index, interp_weight, neighbour_blocks, tiles)


def solution(mesh):
    in_specs = (
        P(None, "space"),
        P("mem", None, "space"),
        P(None, "space"),
        P(None, "space"),
        P(None, "space"),
        P("space", None, None, None),
    )
    out_specs = P(None, ("space", "mem"))
    return jax.shard_map(shards, mesh=mesh, in_specs=in_specs, out_specs=out_specs, check_vma=False)
```

```python
import jax
import jax.numpy as jnp
from jax import lax
from jax.experimental import pallas as pl
from jax.experimental.pallas import tpu as pltpu
from jax.sharding import PartitionSpec as P

MESH = pl.DeviceIdType.MESH
BLOCK = 128
INTP = 3
SUB_DEV = 2048
NB = 9
HB = 8
CB = 512
NCB = 16
WIN = 384
GREET = 2
FIRST = 2
EARLY = 3
F32 = jnp.float32
BF16 = jnp.bfloat16


def dedupe(i0, i1, i2, w0, w1, w2):
    same01, same02, same12 = i0 == i1, i0 == i2, i1 == i2
    zero = jnp.zeros_like(w0)
    none = jnp.full_like(i0, 512.0)
    w0 = w0 + jnp.where(same01, w1, zero) + jnp.where(same02, w2, zero)
    w1 = w1 + jnp.where(same12, w2, zero)
    return i0, jnp.where(same01, none, i1), jnp.where(same02 | same12, none, i2), w0, w1, w2


def build_table(cb, idx_v, wgt_v, table):
    iota = lax.broadcasted_iota(jnp.int32, (16, BLOCK), 0).astype(F32)
    for t in range(CB // BLOCK):
        cols = slice(cb * CB + t * BLOCK, cb * CB + (t + 1) * BLOCK)
        idx = [(idx_v[k : k + 1, cols] - (cb * BLOCK + WIN // 2)).astype(F32) for k in range(INTP)]
        wgt = [wgt_v[k : k + 1, cols] for k in range(INTP)]
        rows = [jnp.broadcast_to(v, (16, BLOCK)).astype(BF16) for v in dedupe(*idx, *wgt)]
        i0, i1, i2, w0, w1, w2 = rows
        for r in range(WIN // 16):
            if r * 16 + 16 <= 32 * t or r * 16 >= 32 * t + 288:
                val = jnp.zeros((16, BLOCK), BF16)
            else:
                point = (iota + (r * 16 - WIN // 2)).astype(BF16)
                val = jnp.where(i2 == point, w2, jnp.zeros((16, BLOCK), BF16))
                val = jnp.where(i1 == point, w1, val)
                val = jnp.where(i0 == point, w0, val)
            table[r * 16 : r * 16 + 16, t * BLOCK : (t + 1) * BLOCK] = val


def kernel(
    n_space,
    n_mem,
    inc_h,
    anom_h,
    idx_h,
    wgt_h,
    nb_h,
    tiles_h,
    out_ref,
    inc_v,
    anom_v,
    idx_v,
    wgt_v,
    nb_s,
    tiles_v,
    table_l,
    table_r,
    spread,
    recv_l,
    recv_r,
    sub,
    smooth,
    part,
    zrecv,
    in_sem,
    send_l_sem,
    send_r_sem,
    recv_l_sem,
    recv_r_sem,
    smooth_send_sem,
    smooth_recv_sem,
    z_send_sem,
    z_recv_sem,
    near_sem,
    far_sem,
):
    me = lax.axis_index("space")
    z = lax.axis_index("mem")
    left, right = me - 1, me + 1
    has_left, has_right = me > 0, me < n_space - 1
    half = NCB // 2

    lo, hi = FIRST * CB, (NCB - FIRST) * CB
    first = [
        pltpu.make_async_copy(idx_h, idx_v, in_sem.at[0]),
        pltpu.make_async_copy(wgt_h, wgt_v, in_sem.at[1]),
        pltpu.make_async_copy(inc_h, inc_v, in_sem.at[2]),
        pltpu.make_async_copy(anom_h.at[:, :lo], anom_v.at[:, :lo], in_sem.at[3]),
        pltpu.make_async_copy(anom_h.at[:, hi:], anom_v.at[:, hi:], in_sem.at[4]),
    ]
    second = pltpu.make_async_copy(anom_h.at[:, lo:hi], anom_v.at[:, lo:hi], in_sem.at[5])
    third = [
        pltpu.make_async_copy(nb_h, nb_s, in_sem.at[6]),
        pltpu.make_async_copy(tiles_h, tiles_v, in_sem.at[7]),
    ]
    for c in (*first, second, *third):
        c.start()

    barrier = pltpu.get_barrier_semaphore()

    def greet(sem, **peer):
        pl.semaphore_signal(sem, inc=1, device_id=peer, device_id_type=MESH)

    def around(step):
        return lax.rem(z + step, n_mem), lax.rem(z + n_mem - step, n_mem)

    for peer in around(1):
        greet(barrier, mem=peer)

    @pl.when(has_left)
    def _():
        greet(barrier, space=left)

    @pl.when(has_right)
    def _():
        greet(barrier, space=right)

    def to_left(k):
        return pltpu.make_async_remote_copy(
            src_ref=spread.at[k],
            dst_ref=recv_r.at[k],
            send_sem=send_l_sem.at[k],
            recv_sem=recv_r_sem.at[k],
            device_id={"space": left},
            device_id_type=MESH,
        )

    def to_right(k):
        return pltpu.make_async_remote_copy(
            src_ref=spread.at[17 - k],
            dst_ref=recv_l.at[k],
            send_sem=send_r_sem.at[k],
            recv_sem=recv_l_sem.at[k],
            device_id={"space": right},
            device_id_type=MESH,
        )

    def send_pair(k):
        @pl.when(has_left)
        def _():
            to_left(k).start()

        @pl.when(has_right)
        def _():
            to_right(k).start()

    def spread_window(cb, table):
        cols = slice(cb * CB, (cb + 1) * CB)
        build_table(cb, idx_v, wgt_v, table)
        inc = inc_v[:, cols].astype(BF16)
        weighted = (anom_v[:, cols].reshape(8, 16, CB) * inc[None]).reshape(128, CB)
        return lax.dot_general(
            weighted, table[...], (((1,), (1,)), ((), ())), preferred_element_type=F32
        )

    for c in first:
        c.wait()
    carry_l = [None, None]
    carry_r = [None, None]
    edge_l, edge_r = [], []

    def plus(a, b):
        return a if b is None else a + b

    for k in range(half):
        if k == FIRST:
            second.wait()
        win_l = spread_window(k, table_l.at[k])
        win_r = spread_window(NCB - 1 - k, table_r.at[k])
        done_l = plus(win_l[:, :128], carry_l[0])
        done_r = plus(win_r[:, 256:], carry_r[0])
        carry_l = [plus(win_l[:, 128:256], carry_l[1]), win_l[:, 256:]]
        carry_r = [plus(win_r[:, 128:256], carry_r[1]), win_r[:, :128]]
        spread[k] = done_l.astype(BF16)
        spread[17 - k] = done_r.astype(BF16)
        if k >= 2:
            sub[7 + k] = done_l.astype(BF16)
            sub[24 - k] = done_r.astype(BF16)
        if k == GREET - 1:
            pl.semaphore_wait(barrier, 2 + has_left.astype(jnp.int32) + has_right.astype(jnp.int32))
            for peer in around(1):
                greet(near_sem, mem=peer)
            for early in range(GREET):
                send_pair(early)
        if k >= GREET:
            send_pair(k)
    mid_l = (carry_l[0] + carry_r[1]).astype(BF16)
    mid_r = (carry_l[1] + carry_r[0]).astype(BF16)
    spread[8] = mid_l
    spread[9] = mid_r
    send_pair(8)
    sub[15] = mid_l
    sub[16] = mid_r

    pl.semaphore_wait(near_sem, 2)
    for peer in around(2):
        greet(far_sem, mem=peer)

    def conv(b):
        picked = jnp.concatenate([sub[nb_s[n, b]] for n in range(NB)], axis=1)
        value = jnp.dot(picked, tiles_v[b], preferred_element_type=F32)
        smooth[1 + b] = value.astype(BF16)

    def z_copy(cb):
        owner, h = cb // 2, cb % 2
        return pltpu.make_async_remote_copy(
            src_ref=part.at[cb],
            dst_ref=zrecv.at[z, h],
            send_sem=z_send_sem.at[cb],
            recv_sem=z_recv_sem.at[z, h],
            device_id={"mem": owner},
            device_id_type=MESH,
        )

    def interp(cb, table):
        window = jnp.concatenate([smooth[cb], smooth[cb + 1], smooth[cb + 2]], axis=1)
        back = jnp.dot(window, table[...], preferred_element_type=F32)
        cols = slice(cb * CB, (cb + 1) * CB)
        prod = back * anom_v[:, cols].astype(F32)
        part[cb] = jnp.sum(prod.reshape(8, 16, CB), axis=0).astype(BF16)

        @pl.when(cb // 2 != z)
        def _():
            z_copy(cb).start()

    def interp_pair(k):
        interp(k, table_l.at[k])
        interp(NCB - 1 - k, table_r.at[k])

    for c in third:
        c.wait()

    def halo(side, copy, own, at, recv, d):
        @pl.when(side)
        def _():
            copy(d).wait_recv()
            if d < 2:
                sub[at] = (own[...].astype(F32) + recv[d].astype(F32)).astype(BF16)
            else:
                sub[at] = recv[d]

        @pl.when(jnp.logical_not(side))
        def _():
            sub[at] = own[...] if d == 0 else jnp.zeros((128, 128), BF16)

    for d in range(half + 1):
        halo(has_left, to_right, spread.at[1 - d] if d < 2 else None, 8 - d, recv_l, d)
        halo(has_right, to_left, spread.at[16 + d] if d < 2 else None, 23 + d, recv_r, d)
        if d >= 1:
            if d == half:
                pl.semaphore_wait(far_sem, 2)
                for s in range(EARLY):
                    interp_pair(half - 1 - s)
            conv(half - d)
            conv(half - 1 + d)

    smooth_left = pltpu.make_async_remote_copy(
        src_ref=smooth.at[1],
        dst_ref=smooth.at[17],
        send_sem=smooth_send_sem.at[0],
        recv_sem=smooth_recv_sem.at[0],
        device_id={"space": left},
        device_id_type=MESH,
    )
    smooth_right = pltpu.make_async_remote_copy(
        src_ref=smooth.at[16],
        dst_ref=smooth.at[0],
        send_sem=smooth_send_sem.at[1],
        recv_sem=smooth_recv_sem.at[1],
        device_id={"space": right},
        device_id_type=MESH,
    )

    @pl.when(has_left)
    def _():
        smooth_left.start()

    @pl.when(has_right)
    def _():
        smooth_right.start()

    for s in range(EARLY, half - 1):
        interp_pair(half - 1 - s)

    @pl.when(has_left)
    def _():
        smooth_right.wait_recv()

    @pl.when(has_right)
    def _():
        smooth_left.wait_recv()

    @pl.when(jnp.logical_not(has_left))
    def _():
        smooth[0] = jnp.zeros((128, 128), BF16)

    @pl.when(jnp.logical_not(has_right))
    def _():
        smooth[17] = jnp.zeros((128, 128), BF16)

    interp_pair(0)

    @pl.when(has_left)
    def _():
        for k in range(9):
            to_left(k).wait_send()
        smooth_left.wait_send()

    @pl.when(has_right)
    def _():
        for k in range(9):
            to_right(k).wait_send()
        smooth_right.wait_send()

    for cb in range(NCB):
        @pl.when(cb // 2 != z)
        def _():
            z_copy(cb).wait_send()

    def z_arrived(source, h):
        return pltpu.make_async_remote_copy(
            src_ref=part.at[0],
            dst_ref=zrecv.at[source, h],
            send_sem=z_send_sem.at[0],
            recv_sem=z_recv_sem.at[source, h],
            device_id={"mem": source},
            device_id_type=MESH,
        )

    for off in range(1, n_mem):
        for h in range(2):
            z_arrived(lax.rem(z + off, n_mem), h).wait_recv()
    for h in range(2):
        total = part[2 * z + h].astype(F32)
        for off in range(1, n_mem):
            total = total + zrecv[lax.rem(z + off, n_mem), h].astype(F32)
        out_ref[:, h * CB : (h + 1) * CB] = total * (1.0 / (8 * n_mem - 1))


def shards(increment, anomalies, interp_index, interp_weight, neighbour_blocks, tiles):
    n_space, n_mem = lax.axis_size("space"), lax.axis_size("mem")
    anomalies = anomalies.reshape(128, NCB * CB)
    tiles = tiles.reshape(16, NB * BLOCK, BLOCK)
    hbm = pl.BlockSpec(memory_space=pl.ANY)
    vmem = pltpu.VMEM
    dma = pltpu.SemaphoreType.DMA
    return pl.pallas_call(
        lambda *refs: kernel(n_space, n_mem, *refs),
        out_shape=jax.ShapeDtypeStruct((16, 2 * CB), F32),
        in_specs=[hbm] * 6,
        out_specs=pl.BlockSpec(memory_space=pltpu.VMEM),
        scratch_shapes=[
            vmem((16, NCB * CB), F32),
            vmem((128, NCB * CB), BF16),
            vmem((INTP, NCB * CB), jnp.int32),
            vmem((INTP, NCB * CB), F32),
            pltpu.SMEM((NB, 16), jnp.int32),
            vmem((16, NB * BLOCK, BLOCK), BF16),
            vmem((8, WIN, CB), BF16),
            vmem((8, WIN, CB), BF16),
            vmem((18, 128, 128), BF16),
            vmem((9, 128, 128), BF16),
            vmem((9, 128, 128), BF16),
            vmem((32, 128, 128), BF16),
            vmem((18, 128, 128), BF16),
            vmem((NCB, 16, CB), BF16),
            vmem((8, 2, 16, CB), BF16),
            dma((8,)),
            dma((9,)),
            dma((9,)),
            dma((9,)),
            dma((9,)),
            dma((2,)),
            dma((2,)),
            dma((NCB,)),
            dma((8, 2)),
            pltpu.SemaphoreType.REGULAR,
            pltpu.SemaphoreType.REGULAR,
        ],
        compiler_params=pltpu.CompilerParams(
            collective_id=0, has_side_effects=True, vmem_limit_bytes=67_043_328
        ),
        name="nicas",
    )(increment, anomalies, interp_index, interp_weight, neighbour_blocks, tiles)


def solution(mesh):
    in_specs = (
        P(None, "space"),
        P("mem", None, "space"),
        P(None, "space"),
        P(None, "space"),
        P(None, "space"),
        P("space", None, None, None),
    )
    out_specs = P(None, ("space", "mem"))
    return jax.shard_map(shards, mesh=mesh, in_specs=in_specs, out_specs=out_specs, check_vma=False)
```

```python
import jax
import jax.numpy as jnp
from jax import lax
from jax.experimental import pallas as pl
from jax.experimental.pallas import tpu as pltpu
from jax.sharding import PartitionSpec as P

MESH = pl.DeviceIdType.MESH
BLOCK = 128
INTP = 3
SUB_DEV = 2048
NB = 9
CB = 512
NCB = 16
CP = 2 * CB
WIN = 512
BAND = 288
FIRST = 2
EARLY = 3
VMEM_LIMIT = 67_043_328 - 190 * 1024
F32 = jnp.float32
BF16 = jnp.bfloat16


def dedupe(i0, i1, i2, w0, w1, w2):
    same01, same02, same12 = i0 == i1, i0 == i2, i1 == i2
    zero = jnp.zeros_like(w0)
    none = jnp.full_like(i0, 512.0)
    w0 = w0 + jnp.where(same01, w1, zero) + jnp.where(same02, w2, zero)
    w1 = w1 + jnp.where(same12, w2, zero)
    return i0, jnp.where(same01, none, i1), jnp.where(same02 | same12, none, i2), w0, w1, w2


def band(t):
    return range(2 * t, 2 * t + BAND // 16)


def clear_table(table):
    for t in range(0, CP // BLOCK, 2):
        lanes = slice(t * BLOCK, (t + 2) * BLOCK)
        low, high = 32 * t, 32 * t + BAND + 32
        if low:
            table[0:low, lanes] = jnp.zeros((low, 2 * BLOCK), BF16)
        if high < WIN:
            table[high:WIN, lanes] = jnp.zeros((WIN - high, 2 * BLOCK), BF16)


def build_table(cb, idx_v, wgt_v, table):
    iota = lax.broadcasted_iota(jnp.int32, (16, BLOCK), 0).astype(F32)
    zero = jnp.zeros((16, BLOCK), BF16)
    for t in range(0, CP // BLOCK, 2):
        rows = []
        for u in (t, t + 1):
            cols = slice(cb * CB + u * BLOCK, cb * CB + (u + 1) * BLOCK)
            idx = [(idx_v[k : k + 1, cols] - (cb * BLOCK + WIN // 2)).astype(F32) for k in range(INTP)]
            wgt = [wgt_v[k : k + 1, cols] for k in range(INTP)]
            rows.append([jnp.broadcast_to(v, (16, BLOCK)).astype(BF16) for v in dedupe(*idx, *wgt)])
        for r in range(2 * t, 2 * t + BAND // 16 + 2):
            point = (iota + (r * 16 - WIN // 2)).astype(BF16)
            vals = []
            for u, (i0, i1, i2, w0, w1, w2) in zip((t, t + 1), rows):
                val = zero
                if r in band(u):
                    val = jnp.where(i2 == point, w2, zero)
                    val = jnp.where(i1 == point, w1, val)
                    val = jnp.where(i0 == point, w0, val)
                vals.append(val)
            table[r * 16 : r * 16 + 16, t * BLOCK : (t + 2) * BLOCK] = jnp.concatenate(vals, axis=1)


def kernel(
    n_space,
    n_mem,
    inc_h,
    anom_h,
    idx_h,
    wgt_h,
    nb_h,
    tiles_h,
    out_ref,
    inc_v,
    anom_v,
    idx_v,
    wgt_v,
    nb_s,
    tiles_v,
    table_l,
    table_r,
    spread,
    recv_l,
    recv_r,
    sub,
    smooth,
    part,
    zrecv,
    in_sem,
    recv_l_sem,
    recv_r_sem,
    smooth_sem,
    out_sem,
    near_sem,
    far_sem,
):
    me = lax.axis_index("space")
    z = lax.axis_index("mem")
    left, right = me - 1, me + 1
    has_left, has_right = me > 0, me < n_space - 1
    steps = NCB // 4

    barrier = pltpu.get_barrier_semaphore()

    def greet(sem, **peer):
        pl.semaphore_signal(sem, inc=1, device_id=peer, device_id_type=MESH)

    def around(step):
        return lax.rem(z + step, n_mem), lax.rem(z + n_mem - step, n_mem)

    lo, hi = FIRST * CB, (NCB - FIRST) * CB
    first = [
        pltpu.make_async_copy(idx_h, idx_v, in_sem.at[0]),
        pltpu.make_async_copy(wgt_h, wgt_v, in_sem.at[1]),
        pltpu.make_async_copy(inc_h, inc_v, in_sem.at[2]),
        pltpu.make_async_copy(anom_h.at[:, :lo], anom_v.at[:, :lo], in_sem.at[3]),
        pltpu.make_async_copy(anom_h.at[:, hi:], anom_v.at[:, hi:], in_sem.at[4]),
    ]
    second = pltpu.make_async_copy(anom_h.at[:, lo:hi], anom_v.at[:, lo:hi], in_sem.at[5])
    third = [
        pltpu.make_async_copy(nb_h, nb_s, in_sem.at[6]),
        pltpu.make_async_copy(tiles_h, tiles_v, in_sem.at[7]),
    ]
    for c in (*first, second, *third):
        c.start()

    for peer in around(1):
        greet(barrier, mem=peer)

    @pl.when(has_left)
    def _():
        greet(barrier, space=left)

    @pl.when(has_right)
    def _():
        greet(barrier, space=right)

    for i in range(steps):
        clear_table(table_l.at[i])
        clear_table(table_r.at[i])

    def size(i):
        return 2 if i < steps else 1

    def to_left(i):
        blocks = pl.ds(2 * i, size(i))
        return pltpu.make_async_remote_copy(
            src_ref=spread.at[blocks],
            dst_ref=recv_r.at[blocks],
            send_sem=out_sem.at[0],
            recv_sem=recv_r_sem.at[i],
            device_id={"space": left},
            device_id_type=MESH,
        )

    def to_right(i):
        low = 18 - 2 * i - size(i)
        return pltpu.make_async_remote_copy(
            src_ref=spread.at[pl.ds(low, size(i))],
            dst_ref=recv_l.at[pl.ds(low - 9, size(i))],
            send_sem=out_sem.at[1],
            recv_sem=recv_l_sem.at[i],
            device_id={"space": right},
            device_id_type=MESH,
        )

    def send_pair(i):
        @pl.when(has_left)
        def _():
            to_left(i).start()

        @pl.when(has_right)
        def _():
            to_right(i).start()

    def spread_window(cb, table):
        cols = slice(cb * CB, cb * CB + CP)
        build_table(cb, idx_v, wgt_v, table)
        inc = inc_v[:, cols].astype(BF16)
        weighted = (anom_v[:, cols].reshape(8, 16, CP) * inc[None]).reshape(128, CP)
        return [
            lax.dot_general(
                weighted,
                table[h * 256 : (h + 1) * 256, :],
                (((1,), (1,)), ((), ())),
                preferred_element_type=F32,
            )
            for h in range(2)
        ]

    for c in first:
        c.wait()
    carry_l = carry_r = None

    def plus(a, b):
        return a if b is None else a + b

    for i in range(steps):
        if i == FIRST // 2:
            second.wait()
        win_l = spread_window(2 * i, table_l.at[i])
        win_r = spread_window(NCB - 2 - 2 * i, table_r.at[i])
        done_l = plus(win_l[0], carry_l).astype(BF16)
        done_r = plus(win_r[1], carry_r).astype(BF16)
        carry_l, carry_r = win_l[1], win_r[0]
        for h in range(2):
            lanes = slice(h * 128, (h + 1) * 128)
            spread[2 * i + h] = done_l[:, lanes]
            spread[16 - 2 * i + h] = done_r[:, lanes]
            if i:
                sub[7 + 2 * i + h] = done_l[:, lanes]
                sub[23 - 2 * i + h] = done_r[:, lanes]
        if i == 0:
            pl.semaphore_wait(barrier, 2 + has_left.astype(jnp.int32) + has_right.astype(jnp.int32))
            for peer in around(1):
                greet(near_sem, mem=peer)
        send_pair(i)
        if i == 2:
            pl.semaphore_wait(near_sem, 2)
            for peer in around(2):
                greet(far_sem, mem=peer)
    mid = (carry_l + carry_r).astype(BF16)
    spread[8] = mid[:, :128]
    spread[9] = mid[:, 128:]
    send_pair(steps)
    sub[15] = mid[:, :128]
    sub[16] = mid[:, 128:]

    def conv_pair(d):
        blocks = (8 - d, 7 + d)
        picked = jnp.concatenate([sub[nb_s[n, b]] for b in blocks for n in range(NB)], axis=1)
        none = jnp.zeros((NB * BLOCK, BLOCK), BF16)
        weights = jnp.concatenate(
            [
                jnp.concatenate([tiles_v[blocks[0]], none], axis=1),
                jnp.concatenate([none, tiles_v[blocks[1]]], axis=1),
            ],
            axis=0,
        )
        value = jnp.dot(picked, weights, preferred_element_type=F32).astype(BF16)
        smooth[1 + blocks[0]] = value[:, :BLOCK]
        smooth[1 + blocks[1]] = value[:, BLOCK:]

    def z_copy(owner, lanes):
        return pltpu.make_async_remote_copy(
            src_ref=part.at[owner, :, lanes],
            dst_ref=zrecv.at[z, :, lanes],
            send_sem=out_sem.at[2],
            recv_sem=out_sem.at[3],
            device_id={"mem": owner},
            device_id_type=MESH,
        )

    def interp(cb):
        i, h = cb // 2, cb % 2
        table = table_l.at[i] if i < steps else table_r.at[2 * steps - 1 - i]
        window = jnp.concatenate([smooth[cb], smooth[cb + 1], smooth[cb + 2]], axis=1)
        weights = table[h * BLOCK : h * BLOCK + 384, h * CB : (h + 1) * CB]
        back = jnp.dot(window, weights, preferred_element_type=F32)
        prod = back * anom_v[:, cb * CB : (cb + 1) * CB].astype(F32)
        part[i, :, h * CB : (h + 1) * CB] = jnp.sum(prod.reshape(8, 16, CB), axis=0).astype(BF16)

    def give(owner, lanes):
        @pl.when(owner != z)
        def _():
            z_copy(owner, lanes).start()

    def interp_step(i):
        for owner in (i, 2 * steps - 1 - i):
            interp(2 * owner)
            interp(2 * owner + 1)
            give(owner, slice(0, CP))

    def interp_half(inner):
        for owner in (0, 2 * steps - 1):
            h = int((owner == 0) == inner)
            interp(2 * owner + h)
            give(owner, slice(h * CB, (h + 1) * CB))

    for c in third:
        c.wait()

    def halo(i):
        for side, copy, recv, at, edge in (
            (has_left, to_right, lambda d: recv_l[8 - d], lambda d: 8 - d, lambda d: spread[1 - d]),
            (has_right, to_left, lambda d: recv_r[d], lambda d: 23 + d, lambda d: spread[16 + d]),
        ):
            span = range(2 * i, 2 * i + size(i))

            @pl.when(side)
            def _():
                copy(i).wait_recv()
                for d in span:
                    if d < 2:
                        sub[at(d)] = (edge(d).astype(F32) + recv(d).astype(F32)).astype(BF16)
                    else:
                        sub[at(d)] = recv(d)

            @pl.when(jnp.logical_not(side))
            def _():
                for d in span:
                    sub[at(d)] = edge(d) if d == 0 else jnp.zeros((128, 128), BF16)

    halo(0)
    conv_pair(1)
    for i in range(1, steps):
        halo(i)
        conv_pair(2 * i)
        conv_pair(2 * i + 1)
    pl.semaphore_wait(far_sem, 2)
    for s in range(EARLY):
        interp_step(steps - 1 - s)
    halo(steps)
    conv_pair(2 * steps)

    smooth_left = pltpu.make_async_remote_copy(
        src_ref=smooth.at[1],
        dst_ref=smooth.at[17],
        send_sem=out_sem.at[0],
        recv_sem=smooth_sem.at[0],
        device_id={"space": left},
        device_id_type=MESH,
    )
    smooth_right = pltpu.make_async_remote_copy(
        src_ref=smooth.at[16],
        dst_ref=smooth.at[0],
        send_sem=out_sem.at[1],
        recv_sem=smooth_sem.at[1],
        device_id={"space": right},
        device_id_type=MESH,
    )

    @pl.when(has_left)
    def _():
        smooth_left.start()

    @pl.when(has_right)
    def _():
        smooth_right.start()

    for s in range(EARLY, steps - 1):
        interp_step(steps - 1 - s)
    interp_half(True)

    @pl.when(has_left)
    def _():
        smooth_right.wait_recv()

    @pl.when(has_right)
    def _():
        smooth_left.wait_recv()

    @pl.when(jnp.logical_not(has_left))
    def _():
        smooth[0] = jnp.zeros((128, 128), BF16)

    @pl.when(jnp.logical_not(has_right))
    def _():
        smooth[17] = jnp.zeros((128, 128), BF16)

    interp_half(False)

    def sent(blocks, sem, **peer):
        return pltpu.make_async_remote_copy(
            src_ref=blocks,
            dst_ref=blocks,
            send_sem=out_sem.at[sem],
            recv_sem=out_sem.at[3],
            device_id=peer,
            device_id_type=MESH,
        )

    @pl.when(has_left)
    def _():
        sent(spread.at[0:10], 0, space=left).wait_send()

    @pl.when(has_right)
    def _():
        sent(spread.at[0:10], 1, space=right).wait_send()

    others = sent(zrecv.at[0 : 2 * steps - 1], 2, mem=lax.rem(z + 1, n_mem))
    others.wait_send()
    others.wait_recv()
    total = part[z].astype(F32)
    for off in range(1, n_mem):
        total = total + zrecv[lax.rem(z + off, n_mem)].astype(F32)
    out_ref[...] = total


def shards(increment, anomalies, interp_index, interp_weight, neighbour_blocks, tiles):
    n_space, n_mem = lax.axis_size("space"), lax.axis_size("mem")
    anomalies = anomalies.reshape(128, NCB * CB)
    tiles = tiles.reshape(16, NB * BLOCK, BLOCK)
    hbm = pl.BlockSpec(memory_space=pl.ANY)
    vmem = pltpu.VMEM
    dma = pltpu.SemaphoreType.DMA
    summed = pl.pallas_call(
        lambda *refs: kernel(n_space, n_mem, *refs),
        out_shape=pltpu.VMEM((16, CP), F32),
        in_specs=[hbm] * 6,
        out_specs=pl.BlockSpec(memory_space=pltpu.VMEM),
        scratch_shapes=[
            vmem((16, NCB * CB), F32),
            vmem((128, NCB * CB), BF16),
            vmem((INTP, NCB * CB), jnp.int32),
            vmem((INTP, NCB * CB), F32),
            pltpu.SMEM((NB, 16), jnp.int32),
            vmem((16, NB * BLOCK, BLOCK), BF16),
            vmem((4, WIN, CP), BF16),
            vmem((4, WIN, CP), BF16),
            vmem((18, 128, 128), BF16),
            vmem((9, 128, 128), BF16),
            vmem((9, 128, 128), BF16),
            vmem((32, 128, 128), BF16),
            vmem((18, 128, 128), BF16),
            vmem((8, 16, CP), BF16),
            vmem((8, 16, CP), BF16),
            dma((8,)),
            dma((5,)),
            dma((5,)),
            dma((2,)),
            dma((4,)),
            pltpu.SemaphoreType.REGULAR,
            pltpu.SemaphoreType.REGULAR,
        ],
        compiler_params=pltpu.CompilerParams(
            collective_id=0, has_side_effects=True, vmem_limit_bytes=VMEM_LIMIT
        ),
        name="nicas",
    )(increment, anomalies, interp_index, interp_weight, neighbour_blocks, tiles)
    return summed / (8 * n_mem - 1)


def solution(mesh):
    in_specs = (
        P(None, "space"),
        P("mem", None, "space"),
        P(None, "space"),
        P(None, "space"),
        P(None, "space"),
        P("space", None, None, None),
    )
    out_specs = P(None, ("space", "mem"))
    return jax.shard_map(shards, mesh=mesh, in_specs=in_specs, out_specs=out_specs, check_vma=False)
```

```python
import jax
import jax.numpy as jnp
from jax import lax
from jax.experimental import pallas as pl
from jax.experimental.pallas import tpu as pltpu
from jax.sharding import PartitionSpec as P

MESH = pl.DeviceIdType.MESH
BLOCK = 128
INTP = 3
SUB_DEV = 2048
NB = 9
CB = 512
NCB = 16
CP = 2 * CB
WIN = 512
BAND = 288
FIRST = 2
VMEM_LIMIT = 67_043_328 - 190 * 1024
F32 = jnp.float32
BF16 = jnp.bfloat16


def dedupe(i0, i1, i2, w0, w1, w2):
    same01, same02, same12 = i0 == i1, i0 == i2, i1 == i2
    zero = jnp.zeros_like(w0)
    none = jnp.full_like(i0, 512.0)
    w0 = w0 + jnp.where(same01, w1, zero) + jnp.where(same02, w2, zero)
    w1 = w1 + jnp.where(same12, w2, zero)
    return i0, jnp.where(same01, none, i1), jnp.where(same02 | same12, none, i2), w0, w1, w2


def band(t):
    return range(2 * t, 2 * t + BAND // 16)


def clear_table(table):
    for t in range(0, CP // BLOCK, 2):
        lanes = slice(t * BLOCK, (t + 2) * BLOCK)
        low, high = 32 * t, 32 * t + BAND + 32
        if low:
            table[0:low, lanes] = jnp.zeros((low, 2 * BLOCK), BF16)
        if high < WIN:
            table[high:WIN, lanes] = jnp.zeros((WIN - high, 2 * BLOCK), BF16)


def build_table(cb, idx_v, wgt_v, table):
    iota = lax.broadcasted_iota(jnp.int32, (16, BLOCK), 0).astype(F32)
    zero = jnp.zeros((16, BLOCK), BF16)
    for t in range(0, CP // BLOCK, 2):
        rows = []
        for u in (t, t + 1):
            cols = slice(cb * CB + u * BLOCK, cb * CB + (u + 1) * BLOCK)
            idx = [(idx_v[k : k + 1, cols] - (cb * BLOCK + WIN // 2)).astype(F32) for k in range(INTP)]
            wgt = [wgt_v[k : k + 1, cols] for k in range(INTP)]
            rows.append([jnp.broadcast_to(v, (16, BLOCK)).astype(BF16) for v in dedupe(*idx, *wgt)])
        for r in range(2 * t, 2 * t + BAND // 16 + 2):
            point = (iota + (r * 16 - WIN // 2)).astype(BF16)
            vals = []
            for u, (i0, i1, i2, w0, w1, w2) in zip((t, t + 1), rows):
                val = zero
                if r in band(u):
                    val = jnp.where(i2 == point, w2, zero)
                    val = jnp.where(i1 == point, w1, val)
                    val = jnp.where(i0 == point, w0, val)
                vals.append(val)
            table[r * 16 : r * 16 + 16, t * BLOCK : (t + 2) * BLOCK] = jnp.concatenate(vals, axis=1)


def kernel(
    n_space,
    n_mem,
    inc_h,
    anom_h,
    idx_h,
    wgt_h,
    nb_h,
    tiles_h,
    out_ref,
    inc_v,
    anom_v,
    idx_v,
    wgt_v,
    nb_s,
    tiles_v,
    table_l,
    table_r,
    spread,
    recv_l,
    recv_r,
    sub,
    smooth,
    part,
    zrecv,
    in_sem,
    recv_l_sem,
    recv_r_sem,
    smooth_sem,
    out_sem,
    far_sem,
):
    me = lax.axis_index("space")
    z = lax.axis_index("mem")
    left, right = me - 1, me + 1
    has_left, has_right = me > 0, me < n_space - 1
    steps = NCB // 4

    barrier = pltpu.get_barrier_semaphore()

    def greet(sem, **peer):
        pl.semaphore_signal(sem, inc=1, device_id=peer, device_id_type=MESH)

    def around(step):
        return lax.rem(z + step, n_mem), lax.rem(z + n_mem - step, n_mem)

    lo, hi = FIRST * CB, (NCB - FIRST) * CB
    first = [
        pltpu.make_async_copy(idx_h, idx_v, in_sem.at[0]),
        pltpu.make_async_copy(wgt_h, wgt_v, in_sem.at[1]),
        pltpu.make_async_copy(inc_h, inc_v, in_sem.at[2]),
        pltpu.make_async_copy(anom_h.at[:, :lo], anom_v.at[:, :lo], in_sem.at[3]),
        pltpu.make_async_copy(anom_h.at[:, hi:], anom_v.at[:, hi:], in_sem.at[4]),
    ]
    second = pltpu.make_async_copy(anom_h.at[:, lo:hi], anom_v.at[:, lo:hi], in_sem.at[5])
    third = [
        pltpu.make_async_copy(nb_h, nb_s, in_sem.at[6]),
        pltpu.make_async_copy(tiles_h, tiles_v, in_sem.at[7]),
    ]
    for c in (*first, second, *third):
        c.start()

    for step in (1, 2):
        for peer in around(step):
            greet(barrier, mem=peer)

    @pl.when(has_left)
    def _():
        greet(barrier, space=left)

    @pl.when(has_right)
    def _():
        greet(barrier, space=right)

    for i in range(steps):
        clear_table(table_l.at[i])
        clear_table(table_r.at[i])

    def size(i):
        return 2 if i < steps else 1

    def to_left(i):
        blocks = pl.ds(2 * i, size(i))
        return pltpu.make_async_remote_copy(
            src_ref=spread.at[blocks],
            dst_ref=recv_r.at[blocks],
            send_sem=out_sem.at[0],
            recv_sem=recv_r_sem.at[i],
            device_id={"space": left},
            device_id_type=MESH,
        )

    def to_right(i):
        low = 18 - 2 * i - size(i)
        return pltpu.make_async_remote_copy(
            src_ref=spread.at[pl.ds(low, size(i))],
            dst_ref=recv_l.at[pl.ds(low - 9, size(i))],
            send_sem=out_sem.at[1],
            recv_sem=recv_l_sem.at[i],
            device_id={"space": right},
            device_id_type=MESH,
        )

    def send_pair(i):
        @pl.when(has_left)
        def _():
            to_left(i).start()

        @pl.when(has_right)
        def _():
            to_right(i).start()

    def spread_window(cb, table):
        cols = slice(cb * CB, cb * CB + CP)
        build_table(cb, idx_v, wgt_v, table)
        inc = inc_v[:, cols].astype(BF16)
        weighted = (anom_v[:, cols].reshape(8, 16, CP) * inc[None]).reshape(128, CP)
        return [
            lax.dot_general(
                weighted,
                table[h * 256 : (h + 1) * 256, :],
                (((1,), (1,)), ((), ())),
                preferred_element_type=F32,
            )
            for h in range(2)
        ]

    for c in first:
        c.wait()
    carry_l = carry_r = None

    def plus(a, b):
        return a if b is None else a + b

    for i in range(steps):
        if i == FIRST // 2:
            second.wait()
        win_l = spread_window(2 * i, table_l.at[i])
        win_r = spread_window(NCB - 2 - 2 * i, table_r.at[i])
        done_l = plus(win_l[0], carry_l).astype(BF16)
        done_r = plus(win_r[1], carry_r).astype(BF16)
        carry_l, carry_r = win_l[1], win_r[0]
        for h in range(2):
            lanes = slice(h * 128, (h + 1) * 128)
            spread[2 * i + h] = done_l[:, lanes]
            spread[16 - 2 * i + h] = done_r[:, lanes]
            if i:
                sub[7 + 2 * i + h] = done_l[:, lanes]
                sub[23 - 2 * i + h] = done_r[:, lanes]
        if i == 0:
            pl.semaphore_wait(barrier, 4 + has_left.astype(jnp.int32) + has_right.astype(jnp.int32))
            for peer in around(2):
                greet(far_sem, mem=peer)
        send_pair(i)
    mid = (carry_l + carry_r).astype(BF16)
    spread[8] = mid[:, :128]
    spread[9] = mid[:, 128:]
    send_pair(steps)
    sub[15] = mid[:, :128]
    sub[16] = mid[:, 128:]

    def conv_pair(d):
        blocks = (8 - d, 7 + d)
        picked = jnp.concatenate([sub[nb_s[n, b]] for b in blocks for n in range(NB)], axis=1)
        none = jnp.zeros((NB * BLOCK, BLOCK), BF16)
        weights = jnp.concatenate(
            [
                jnp.concatenate([tiles_v[blocks[0]], none], axis=1),
                jnp.concatenate([none, tiles_v[blocks[1]]], axis=1),
            ],
            axis=0,
        )
        value = jnp.dot(picked, weights, preferred_element_type=F32).astype(BF16)
        smooth[1 + blocks[0]] = value[:, :BLOCK]
        smooth[1 + blocks[1]] = value[:, BLOCK:]

    def z_copy(owner, lanes):
        return pltpu.make_async_remote_copy(
            src_ref=part.at[owner, :, lanes],
            dst_ref=zrecv.at[z, :, lanes],
            send_sem=out_sem.at[2],
            recv_sem=out_sem.at[3],
            device_id={"mem": owner},
            device_id_type=MESH,
        )

    def interp(cb):
        i, h = cb // 2, cb % 2
        table = table_l.at[i] if i < steps else table_r.at[2 * steps - 1 - i]
        window = jnp.concatenate([smooth[cb], smooth[cb + 1], smooth[cb + 2]], axis=1)
        weights = table[h * BLOCK : h * BLOCK + 384, h * CB : (h + 1) * CB]
        back = jnp.dot(window, weights, preferred_element_type=F32)
        prod = back * anom_v[:, cb * CB : (cb + 1) * CB].astype(F32)
        part[i, :, h * CB : (h + 1) * CB] = jnp.sum(prod.reshape(8, 16, CB), axis=0).astype(BF16)

    def give(owner, lanes):
        @pl.when(owner != z)
        def _():
            z_copy(owner, lanes).start()

    def interp_step(i):
        for owner in (i, 2 * steps - 1 - i):
            interp(2 * owner)
            interp(2 * owner + 1)

    def give_step(i):
        for owner in (i, 2 * steps - 1 - i):
            give(owner, slice(0, CP))

    def interp_half(inner):
        for owner in (0, 2 * steps - 1):
            h = int((owner == 0) == inner)
            interp(2 * owner + h)
            give(owner, slice(h * CB, (h + 1) * CB))

    for c in third:
        c.wait()

    def halo(i):
        for side, copy, recv, at, edge in (
            (has_left, to_right, lambda d: recv_l[8 - d], lambda d: 8 - d, lambda d: spread[1 - d]),
            (has_right, to_left, lambda d: recv_r[d], lambda d: 23 + d, lambda d: spread[16 + d]),
        ):
            span = range(2 * i, 2 * i + size(i))

            @pl.when(side)
            def _():
                copy(i).wait_recv()
                for d in span:
                    if d < 2:
                        sub[at(d)] = (edge(d).astype(F32) + recv(d).astype(F32)).astype(BF16)
                    else:
                        sub[at(d)] = recv(d)

            @pl.when(jnp.logical_not(side))
            def _():
                for d in span:
                    sub[at(d)] = edge(d) if d == 0 else jnp.zeros((128, 128), BF16)

    halo(0)
    conv_pair(1)
    for i in range(1, steps - 1):
        halo(i)
        conv_pair(2 * i)
        conv_pair(2 * i + 1)
    interp_step(3)
    interp_step(2)
    pl.semaphore_wait(far_sem, 2)
    give_step(3)
    give_step(2)
    halo(steps - 1)
    halo(steps)
    conv_pair(2 * steps)

    smooth_left = pltpu.make_async_remote_copy(
        src_ref=smooth.at[1],
        dst_ref=smooth.at[17],
        send_sem=out_sem.at[0],
        recv_sem=smooth_sem.at[0],
        device_id={"space": left},
        device_id_type=MESH,
    )
    smooth_right = pltpu.make_async_remote_copy(
        src_ref=smooth.at[16],
        dst_ref=smooth.at[0],
        send_sem=out_sem.at[1],
        recv_sem=smooth_sem.at[1],
        device_id={"space": right},
        device_id_type=MESH,
    )

    @pl.when(has_left)
    def _():
        smooth_left.start()

    @pl.when(has_right)
    def _():
        smooth_right.start()

    conv_pair(2 * steps - 2)
    conv_pair(2 * steps - 1)
    interp_step(1)
    give_step(1)
    interp_half(True)

    @pl.when(has_left)
    def _():
        smooth_right.wait_recv()

    @pl.when(has_right)
    def _():
        smooth_left.wait_recv()

    @pl.when(jnp.logical_not(has_left))
    def _():
        smooth[0] = jnp.zeros((128, 128), BF16)

    @pl.when(jnp.logical_not(has_right))
    def _():
        smooth[17] = jnp.zeros((128, 128), BF16)

    interp_half(False)

    def sent(blocks, sem, **peer):
        return pltpu.make_async_remote_copy(
            src_ref=blocks,
            dst_ref=blocks,
            send_sem=out_sem.at[sem],
            recv_sem=out_sem.at[3],
            device_id=peer,
            device_id_type=MESH,
        )

    @pl.when(has_left)
    def _():
        sent(spread.at[0:10], 0, space=left).wait_send()

    @pl.when(has_right)
    def _():
        sent(spread.at[0:10], 1, space=right).wait_send()

    others = sent(zrecv.at[0 : 2 * steps - 1], 2, mem=lax.rem(z + 1, n_mem))
    others.wait_send()
    others.wait_recv()
    total = part[z].astype(F32)
    for off in range(1, n_mem):
        total = total + zrecv[lax.rem(z + off, n_mem)].astype(F32)
    out_ref[...] = total


def shards(increment, anomalies, interp_index, interp_weight, neighbour_blocks, tiles):
    n_space, n_mem = lax.axis_size("space"), lax.axis_size("mem")
    anomalies = anomalies.reshape(128, NCB * CB)
    tiles = tiles.reshape(16, NB * BLOCK, BLOCK)
    hbm = pl.BlockSpec(memory_space=pl.ANY)
    vmem = pltpu.VMEM
    dma = pltpu.SemaphoreType.DMA
    summed = pl.pallas_call(
        lambda *refs: kernel(n_space, n_mem, *refs),
        out_shape=pltpu.VMEM((16, CP), F32),
        in_specs=[hbm] * 6,
        out_specs=pl.BlockSpec(memory_space=pltpu.VMEM),
        scratch_shapes=[
            vmem((16, NCB * CB), F32),
            vmem((128, NCB * CB), BF16),
            vmem((INTP, NCB * CB), jnp.int32),
            vmem((INTP, NCB * CB), F32),
            pltpu.SMEM((NB, 16), jnp.int32),
            vmem((16, NB * BLOCK, BLOCK), BF16),
            vmem((4, WIN, CP), BF16),
            vmem((4, WIN, CP), BF16),
            vmem((18, 128, 128), BF16),
            vmem((9, 128, 128), BF16),
            vmem((9, 128, 128), BF16),
            vmem((32, 128, 128), BF16),
            vmem((18, 128, 128), BF16),
            vmem((8, 16, CP), BF16),
            vmem((8, 16, CP), BF16),
            dma((8,)),
            dma((5,)),
            dma((5,)),
            dma((2,)),
            dma((4,)),
            pltpu.SemaphoreType.REGULAR,
        ],
        compiler_params=pltpu.CompilerParams(
            collective_id=0, has_side_effects=True, vmem_limit_bytes=VMEM_LIMIT
        ),
        name="nicas",
    )(increment, anomalies, interp_index, interp_weight, neighbour_blocks, tiles)
    return summed / (8 * n_mem - 1)


def solution(mesh):
    in_specs = (
        P(None, "space"),
        P("mem", None, "space"),
        P(None, "space"),
        P(None, "space"),
        P(None, "space"),
        P("space", None, None, None),
    )
    out_specs = P(None, ("space", "mem"))
    return jax.shard_map(shards, mesh=mesh, in_specs=in_specs, out_specs=out_specs, check_vma=False)
```

```python
import jax
import jax.numpy as jnp
from jax import lax
from jax.experimental import pallas as pl
from jax.experimental.pallas import tpu as pltpu
from jax.sharding import PartitionSpec as P

MESH = pl.DeviceIdType.MESH
BLOCK = 128
INTP = 3
SUB_DEV = 2048
NB = 9
CB = 512
NCB = 16
CP = 2 * CB
WIN = 512
BAND = 288
FIRST = 2
VMEM_LIMIT = 67_043_328 - 190 * 1024
F32 = jnp.float32
BF16 = jnp.bfloat16


def dedupe(i0, i1, i2, w0, w1, w2):
    same01, same02, same12 = i0 == i1, i0 == i2, i1 == i2
    zero = jnp.zeros_like(w0)
    none = jnp.full_like(i0, 512.0)
    w0 = w0 + jnp.where(same01, w1, zero) + jnp.where(same02, w2, zero)
    w1 = w1 + jnp.where(same12, w2, zero)
    return i0, jnp.where(same01, none, i1), jnp.where(same02 | same12, none, i2), w0, w1, w2


def band(t):
    return range(2 * t, 2 * t + BAND // 16)


def clear_table(table):
    for t in range(0, CP // BLOCK, 2):
        lanes = slice(t * BLOCK, (t + 2) * BLOCK)
        low, high = 32 * t, 32 * t + BAND + 32
        if low:
            table[0:low, lanes] = jnp.zeros((low, 2 * BLOCK), BF16)
        if high < WIN:
            table[high:WIN, lanes] = jnp.zeros((WIN - high, 2 * BLOCK), BF16)


def build_table(cb, idx_v, wgt_v, table):
    iota = lax.broadcasted_iota(jnp.int32, (16, BLOCK), 0).astype(F32)
    zero = jnp.zeros((16, BLOCK), BF16)
    for t in range(0, CP // BLOCK, 2):
        rows = []
        for u in (t, t + 1):
            cols = slice(cb * CB + u * BLOCK, cb * CB + (u + 1) * BLOCK)
            idx = [(idx_v[k : k + 1, cols] - (cb * BLOCK + WIN // 2)).astype(F32) for k in range(INTP)]
            wgt = [wgt_v[k : k + 1, cols] for k in range(INTP)]
            rows.append([jnp.broadcast_to(v, (16, BLOCK)).astype(BF16) for v in dedupe(*idx, *wgt)])
        for r in range(2 * t, 2 * t + BAND // 16 + 2):
            point = (iota + (r * 16 - WIN // 2)).astype(BF16)
            vals = []
            for u, (i0, i1, i2, w0, w1, w2) in zip((t, t + 1), rows):
                val = zero
                if r in band(u):
                    val = jnp.where(i2 == point, w2, zero)
                    val = jnp.where(i1 == point, w1, val)
                    val = jnp.where(i0 == point, w0, val)
                vals.append(val)
            table[r * 16 : r * 16 + 16, t * BLOCK : (t + 2) * BLOCK] = jnp.concatenate(vals, axis=1)


def kernel(
    n_space,
    n_mem,
    inc_h,
    anom_h,
    idx_h,
    wgt_h,
    nb_h,
    tiles_h,
    out_ref,
    inc_v,
    anom_v,
    idx_v,
    wgt_v,
    nb_s,
    tiles_v,
    table_l,
    table_r,
    spread,
    recv_l,
    recv_r,
    sub,
    smooth,
    part,
    zrecv,
    in_sem,
    recv_l_sem,
    recv_r_sem,
    smooth_sem,
    out_sem,
):
    me = lax.axis_index("space")
    z = lax.axis_index("mem")
    left, right = me - 1, me + 1
    has_left, has_right = me > 0, me < n_space - 1
    steps = NCB // 4

    barrier = pltpu.get_barrier_semaphore()

    def greet(sem, **peer):
        pl.semaphore_signal(sem, inc=1, device_id=peer, device_id_type=MESH)

    def columns(src, dst, low, high, sem):
        cols = slice(low * CB, high * CB)
        return pltpu.make_async_copy(src.at[:, cols], dst.at[:, cols], in_sem.at[sem])

    def fields(low, high, sem):
        return [
            columns(inc_h, inc_v, low, high, sem),
            columns(anom_h, anom_v, low, high, sem + 1),
        ]

    where = [
        pltpu.make_async_copy(idx_h, idx_v, in_sem.at[0]),
        pltpu.make_async_copy(wgt_h, wgt_v, in_sem.at[1]),
    ]
    first_l, first_r = fields(0, FIRST, 2), fields(NCB - FIRST, NCB, 4)
    second = fields(FIRST, NCB - FIRST, 6)
    third = [
        pltpu.make_async_copy(nb_h, nb_s, in_sem.at[8]),
        pltpu.make_async_copy(tiles_h, tiles_v, in_sem.at[9]),
    ]
    for c in (*where, *first_l, *first_r, *second, *third):
        c.start()

    for step in range(1, n_mem):
        greet(barrier, mem=lax.rem(z + step, n_mem))

    @pl.when(has_left)
    def _():
        greet(barrier, space=left)

    @pl.when(has_right)
    def _():
        greet(barrier, space=right)

    for i in range(steps):
        clear_table(table_l.at[i])
        clear_table(table_r.at[i])

    def size(i):
        return 2 if i < steps else 1

    def to_left(i):
        blocks = pl.ds(2 * i, size(i))
        return pltpu.make_async_remote_copy(
            src_ref=spread.at[blocks],
            dst_ref=recv_r.at[blocks],
            send_sem=out_sem.at[0],
            recv_sem=recv_r_sem.at[i],
            device_id={"space": left},
            device_id_type=MESH,
        )

    def to_right(i):
        low = 18 - 2 * i - size(i)
        return pltpu.make_async_remote_copy(
            src_ref=spread.at[pl.ds(low, size(i))],
            dst_ref=recv_l.at[pl.ds(low - 9, size(i))],
            send_sem=out_sem.at[1],
            recv_sem=recv_l_sem.at[i],
            device_id={"space": right},
            device_id_type=MESH,
        )

    def send_pair(i):
        @pl.when(has_left)
        def _():
            to_left(i).start()

        @pl.when(has_right)
        def _():
            to_right(i).start()

    def spread_window(cb, table):
        cols = slice(cb * CB, cb * CB + CP)
        build_table(cb, idx_v, wgt_v, table)
        inc = inc_v[:, cols].astype(BF16)
        weighted = (anom_v[:, cols].reshape(8, 16, CP) * inc[None]).reshape(128, CP)
        return [
            lax.dot_general(
                weighted,
                table[h * 256 : (h + 1) * 256, :],
                (((1,), (1,)), ((), ())),
                preferred_element_type=F32,
            )
            for h in range(2)
        ]

    for c in (*where, *first_l, *first_r):
        c.wait()
    carry_l = carry_r = None

    def plus(a, b):
        return a if b is None else a + b

    for i in range(steps):
        if i == FIRST // 2:
            for c in second:
                c.wait()
        win_l = spread_window(2 * i, table_l.at[i])
        win_r = spread_window(NCB - 2 - 2 * i, table_r.at[i])
        done_l = plus(win_l[0], carry_l).astype(BF16)
        done_r = plus(win_r[1], carry_r).astype(BF16)
        carry_l, carry_r = win_l[1], win_r[0]
        for h in range(2):
            lanes = slice(h * 128, (h + 1) * 128)
            spread[2 * i + h] = done_l[:, lanes]
            spread[16 - 2 * i + h] = done_r[:, lanes]
            if i:
                sub[7 + 2 * i + h] = done_l[:, lanes]
                sub[23 - 2 * i + h] = done_r[:, lanes]
        if i == 0:
            peers = n_mem - 1 + has_left.astype(jnp.int32) + has_right.astype(jnp.int32)
            pl.semaphore_wait(barrier, peers)
        send_pair(i)
    mid = (carry_l + carry_r).astype(BF16)
    spread[8] = mid[:, :128]
    spread[9] = mid[:, 128:]
    send_pair(steps)
    sub[15] = mid[:, :128]
    sub[16] = mid[:, 128:]

    def conv_pair(d):
        blocks = (8 - d, 7 + d)
        picked = jnp.concatenate([sub[nb_s[n, b]] for b in blocks for n in range(NB)], axis=1)
        none = jnp.zeros((NB * BLOCK, BLOCK), BF16)
        weights = jnp.concatenate(
            [
                jnp.concatenate([tiles_v[blocks[0]], none], axis=1),
                jnp.concatenate([none, tiles_v[blocks[1]]], axis=1),
            ],
            axis=0,
        )
        value = jnp.dot(picked, weights, preferred_element_type=F32).astype(BF16)
        smooth[1 + blocks[0]] = value[:, :BLOCK]
        smooth[1 + blocks[1]] = value[:, BLOCK:]

    def z_copy(owner, lanes):
        return pltpu.make_async_remote_copy(
            src_ref=part.at[owner, :, lanes],
            dst_ref=zrecv.at[z, :, lanes],
            send_sem=out_sem.at[2],
            recv_sem=out_sem.at[3],
            device_id={"mem": owner},
            device_id_type=MESH,
        )

    def interp(cb):
        i, h = cb // 2, cb % 2
        table = table_l.at[i] if i < steps else table_r.at[2 * steps - 1 - i]
        window = jnp.concatenate([smooth[cb], smooth[cb + 1], smooth[cb + 2]], axis=1)
        weights = table[h * BLOCK : h * BLOCK + 384, h * CB : (h + 1) * CB]
        back = jnp.dot(window, weights, preferred_element_type=F32)
        prod = back * anom_v[:, cb * CB : (cb + 1) * CB].astype(F32)
        part[i, :, h * CB : (h + 1) * CB] = jnp.sum(prod.reshape(8, 16, CB), axis=0).astype(BF16)

    def give(owner, lanes):
        @pl.when(owner != z)
        def _():
            z_copy(owner, lanes).start()

    def interp_owner(owner):
        interp(2 * owner)
        interp(2 * owner + 1)

    def interp_half(inner):
        for owner in (0, 2 * steps - 1):
            h = int((owner == 0) == inner)
            interp(2 * owner + h)
            give(owner, slice(h * CB, (h + 1) * CB))

    for c in third:
        c.wait()

    def halo(i):
        for side, copy, recv, at, edge in (
            (has_left, to_right, lambda d: recv_l[8 - d], lambda d: 8 - d, lambda d: spread[1 - d]),
            (has_right, to_left, lambda d: recv_r[d], lambda d: 23 + d, lambda d: spread[16 + d]),
        ):
            span = range(2 * i, 2 * i + size(i))

            @pl.when(side)
            def _():
                copy(i).wait_recv()
                for d in span:
                    if d < 2:
                        sub[at(d)] = (edge(d).astype(F32) + recv(d).astype(F32)).astype(BF16)
                    else:
                        sub[at(d)] = recv(d)

            @pl.when(jnp.logical_not(side))
            def _():
                for d in span:
                    sub[at(d)] = edge(d) if d == 0 else jnp.zeros((128, 128), BF16)

    halo(0)
    conv_pair(1)
    for i in range(1, steps - 1):
        halo(i)
        conv_pair(2 * i)
        conv_pair(2 * i + 1)
    inner = (steps - 1, steps, steps - 2, steps + 1)
    for owner in inner:
        interp_owner(owner)
    for owner in inner:
        give(owner, slice(0, CP))
    halo(steps - 1)
    halo(steps)
    conv_pair(2 * steps)

    smooth_left = pltpu.make_async_remote_copy(
        src_ref=smooth.at[1],
        dst_ref=smooth.at[17],
        send_sem=out_sem.at[0],
        recv_sem=smooth_sem.at[0],
        device_id={"space": left},
        device_id_type=MESH,
    )
    smooth_right = pltpu.make_async_remote_copy(
        src_ref=smooth.at[16],
        dst_ref=smooth.at[0],
        send_sem=out_sem.at[1],
        recv_sem=smooth_sem.at[1],
        device_id={"space": right},
        device_id_type=MESH,
    )

    @pl.when(has_left)
    def _():
        smooth_left.start()

    @pl.when(has_right)
    def _():
        smooth_right.start()

    conv_pair(2 * steps - 2)
    conv_pair(2 * steps - 1)
    interp_half(True)
    for owner in (1, 2 * steps - 2):
        interp_owner(owner)
        give(owner, slice(0, CP))

    @pl.when(has_left)
    def _():
        smooth_right.wait_recv()

    @pl.when(has_right)
    def _():
        smooth_left.wait_recv()

    @pl.when(jnp.logical_not(has_left))
    def _():
        smooth[0] = jnp.zeros((128, 128), BF16)

    @pl.when(jnp.logical_not(has_right))
    def _():
        smooth[17] = jnp.zeros((128, 128), BF16)

    interp_half(False)

    def sent(blocks, sem, **peer):
        return pltpu.make_async_remote_copy(
            src_ref=blocks,
            dst_ref=blocks,
            send_sem=out_sem.at[sem],
            recv_sem=out_sem.at[3],
            device_id=peer,
            device_id_type=MESH,
        )

    @pl.when(has_left)
    def _():
        sent(spread.at[0:10], 0, space=left).wait_send()

    @pl.when(has_right)
    def _():
        sent(spread.at[0:10], 1, space=right).wait_send()

    others = sent(zrecv.at[0 : 2 * steps - 1], 2, mem=lax.rem(z + 1, n_mem))
    others.wait_send()
    others.wait_recv()
    total = part[z].astype(F32)
    for off in range(1, n_mem):
        total = total + zrecv[lax.rem(z + off, n_mem)].astype(F32)
    out_ref[...] = total


def shards(increment, anomalies, interp_index, interp_weight, neighbour_blocks, tiles):
    n_space, n_mem = lax.axis_size("space"), lax.axis_size("mem")
    anomalies = anomalies.reshape(128, NCB * CB)
    tiles = tiles.reshape(16, NB * BLOCK, BLOCK)
    hbm = pl.BlockSpec(memory_space=pl.ANY)
    vmem = pltpu.VMEM
    dma = pltpu.SemaphoreType.DMA
    summed = pl.pallas_call(
        lambda *refs: kernel(n_space, n_mem, *refs),
        out_shape=pltpu.VMEM((16, CP), F32),
        in_specs=[hbm] * 6,
        out_specs=pl.BlockSpec(memory_space=pltpu.VMEM),
        scratch_shapes=[
            vmem((16, NCB * CB), F32),
            vmem((128, NCB * CB), BF16),
            vmem((INTP, NCB * CB), jnp.int32),
            vmem((INTP, NCB * CB), F32),
            pltpu.SMEM((NB, 16), jnp.int32),
            vmem((16, NB * BLOCK, BLOCK), BF16),
            vmem((4, WIN, CP), BF16),
            vmem((4, WIN, CP), BF16),
            vmem((18, 128, 128), BF16),
            vmem((9, 128, 128), BF16),
            vmem((9, 128, 128), BF16),
            vmem((32, 128, 128), BF16),
            vmem((18, 128, 128), BF16),
            vmem((8, 16, CP), BF16),
            vmem((8, 16, CP), BF16),
            dma((10,)),
            dma((5,)),
            dma((5,)),
            dma((2,)),
            dma((4,)),
        ],
        compiler_params=pltpu.CompilerParams(
            collective_id=0, has_side_effects=True, vmem_limit_bytes=VMEM_LIMIT
        ),
        name="nicas",
    )(increment, anomalies, interp_index, interp_weight, neighbour_blocks, tiles)
    return summed / (8 * n_mem - 1)


def solution(mesh):
    in_specs = (
        P(None, "space"),
        P("mem", None, "space"),
        P(None, "space"),
        P(None, "space"),
        P(None, "space"),
        P("space", None, None, None),
    )
    out_specs = P(None, ("space", "mem"))
    return jax.shard_map(shards, mesh=mesh, in_specs=in_specs, out_specs=out_specs, check_vma=False)
```
